32 devices in a mesh: parts: 2 (over y), wide: 4 (over z), mp: 4 (over x, core).
Axes of the slice: x: 2, y: 2, z: 4, core: 2. Of those that a mesh axis runs over, the one named last changes fastest.
Arguments:
- prompt_states: bfloat16 [4096, 8192], P(('parts', 'wide'), 'mp'), parts along dimension 0, may hold values from -6 to 6
- norm_gain: float32 [8192], P('mp'), may hold values from 0.1 to 1.9
- kv_weight: bfloat16 [8192, 2048], P('mp', 'wide'), may hold values from -0.0625 to 0.0625
- block_owner: int32 [256, 1], P(('parts', 'wide')), parts along dimension 0, may hold values from 0 to 3; in each aligned block of 32 rows (0 to 31, 32 to 63, ...) at most 16 rows name the same one
- block_request: int32 [256], P(('parts', 'wide')), parts along dimension 0, may hold values from 0 to 1
- block_admit: int32 [256], P(('parts', 'wide')), parts along dimension 0, may hold values 0 or 1
- cache_kv: bfloat16 [16, 2048, 2048], P(('parts', 'wide'), None, 'mp'), parts along dimension 0, may hold values from -6 to 6
- cache_len: int32 [16], P(('parts', 'wide')), parts along dimension 0, may hold values from 1 to 2048
- queries: bfloat16 [16, 4, 8192], P(('parts', 'wide'), None, 'mp'), parts along dimension 0, may hold values from -128 to 128
- draft_kv: bfloat16 [16, 4, 2048], P(('parts', 'wide'), None, 'mp'), parts along dimension 0, may hold values from -8 to 8
Outputs:
- attended: bfloat16 [16, 4, 8192], P(('parts', 'wide'), None, 'mp'), parts along dimension 0
The draws below stay inside these ranges and needn't reach their ends.
There are 2 independent parts, one for each index of `parts`. The reference program is written for one: setup_inputs(seed, part) draws one part's arguments, and reference() takes and returns one part's arrays. A program takes and returns all parts, laid end to end along the dimension named above; an argument that names none is the same for every part. Nothing has to cross between parts.
Inputs may be any that keep to these rules, and one draw needn't show every extreme that they name: `block_owner`: in each prefill group's 32 blocks no owner is named more than 16 times, a bound that some block reaches.
All inputs are finite; a program needn't handle non-finite values. No bound on the sum of `block_admit` on one device may be relied on, other than what follows from the above.
Results may differ from the reference program's by a relative error of at most 0.019.
Values may be sent and summed in bfloat16 or wider, within the bound.
A program may use at most 64 MiB of HBM per device.

```python
import math
import jax
import jax.numpy as jnp
import numpy as np
from jax import lax

D = 8192
KVH = 8
HD = 128
QH = 64
KVW = 2048
BLK = 16
PBLK = 32
CAP = 16
REQ_DEV = 2
CACHE = 2048
STEPS = 4
PTOKENS = 2048
PBLOCKS = 128
REQUESTS = 8
N_WIDE = 4
N_MP = 4


def joint_draw(key):
    base = jax.random.fold_in(key, 7101)
    key_draft, key_query = jax.random.split(base, 2)
    groups = QH // KVH
    draft = jnp.clip(jax.random.normal(key_draft, (REQUESTS, STEPS, KVH, 2, HD), jnp.float32), -6.0, 6.0)
    query = jnp.clip(jax.random.normal(key_query, (REQUESTS, STEPS, KVH, groups, HD), jnp.float32), -6.0, 6.0)
    return (query.reshape(REQUESTS, STEPS, QH * HD), draft.reshape(REQUESTS, STEPS, KVH * 2 * HD))


def draw_queries(key, part):
    return joint_draw(key)[0].astype(jnp.bfloat16)


def draw_draft_kv(key, part):
    return joint_draw(key)[1].astype(jnp.bfloat16)


def with_ends(array, own_key, low, high):
    index_at = [jax.random.randint(jax.random.fold_in(own_key, axis), (), 0, length) for axis, length in enumerate(array.shape)]
    widest = array.shape.index(max(array.shape))
    beside = index_at[:widest] + [(index_at[widest] + 1) % array.shape[widest]] + index_at[widest + 1:]
    return array.at[tuple(index_at)].set(low).at[tuple(beside)].set(high)


def block_scale(key, dims, cuts, smallest, largest):
    factor_of, own = 1.0, jax.random.fold_in(key, 6)
    for dim, shards_of in cuts:
        draws = jnp.exp(jax.random.uniform(jax.random.fold_in(own, dim), (shards_of,), jnp.float32, smallest / len(cuts), largest / len(cuts)))
        factor_of = factor_of * jnp.repeat(draws, dims[dim] // shards_of).reshape([-1 if axis == dim else 1 for axis in range(len(dims))])
    return factor_of


def shared_out(key, own, number, rows, count, top, most, slope):
    ranking = jax.random.permutation(key, count)
    heavy_load, ordinary = shares(count, rows * top, most, slope, True), shares(count, rows * top, most, slope, False)
    places = jnp.arange(count)

    def named(sizes, rotation):
        used = int((sizes > 0).sum())
        fixed = max(1, used // 4)
        moved = fixed + (places - fixed + rotation * (used - fixed)) % max(1, count - fixed)
        return jnp.zeros((count,), jnp.int32).at[ranking[jnp.where(places < fixed, places, moved)]].set(jnp.asarray(sizes, jnp.int32))

    sizes = jnp.where(number % 4 == 0, named(heavy_load, number // 4), named(ordinary, number - number // 4 - 1))
    mixed = jax.random.permutation(jax.random.fold_in(own, 3), count)
    giver, receiver = mixed[0:count // 2 * 2:2], mixed[1:count // 2 * 2:2]
    room = jnp.minimum(sizes[giver] - 1, most - sizes[receiver]) // 2
    room = jnp.where((giver == ranking[0]) | (receiver == ranking[0]) | (sizes[receiver] == 0), 0, jnp.maximum(room, 0))
    moved = jax.random.randint(jax.random.fold_in(own, 4), (count // 2,), 0, 1 << 20) % (room + 1)
    sizes = sizes.at[giver].add(-moved).at[receiver].add(moved)
    items = jnp.searchsorted(jnp.cumsum(sizes), jnp.arange(rows * top), side="right").astype(jnp.int32)
    listing = items.reshape(top, rows).T
    listing = listing[jax.random.permutation(jax.random.fold_in(own, 1), rows)]
    rotation = jax.random.randint(jax.random.fold_in(own, 2), (rows, 1), 0, top)
    return jnp.take_along_axis(listing, (jnp.arange(top)[None, :] + rotation) % top, axis=1)


def shares(count, total, reach, skew, full):
    portions = [(1 << 20) // math.isqrt(grade ** skew) + 1 for grade in range(1, count + 1)]
    largest = reach if full else min(reach, max(-(-total // count), total * portions[0] // sum(portions)))
    least = 1 if total - largest >= count - 1 else 0
    counts, rest = [largest] + [least] * (count - 1), total - largest - least * (count - 1)
    while rest > 0:
        candidates = [i for i in range(1, count) if counts[i] < largest] or [i for i in range(1, count) if counts[i] < reach]
        pool, budget = sum([portions[i] for i in candidates]), rest
        for i in candidates:
            more = min(reach - counts[i], max(1, budget * portions[i] // pool), rest)
            counts[i] = counts[i] + more
            rest = rest - more
    return np.array(counts)


def noise(rng, shape, deviation, limit, pieces=(), kind=jnp.bfloat16):
    values = jax.random.normal(rng, shape, jnp.float32) * deviation
    if len(pieces) > 0:
        values = block_scale(rng, shape, pieces, -0.22, 0.18) * values
    return jnp.clip(values, min=-limit, max=limit).astype(kind)


def setup_inputs(seed: int = 0, part: int = 0) -> dict:
    arg_keys = jax.random.split(jax.random.key(seed), 11)
    part_splits = jax.random.split(jax.random.fold_in(arg_keys[10], part), 11)
    prompt_states = noise(part_splits[0], (PTOKENS, D), 1.0, 6.0, ((0, 4), (1, 4)))
    norm_gain = jnp.clip(1.0 + 0.18 * jax.random.normal(arg_keys[1], (D,), jnp.float32), 0.1, 1.9)
    kv_weight = noise(arg_keys[2], (D, KVW), D ** -0.5, 0.0625, ((0, 4), (1, 4)))
    block_owner_keys = jax.random.split(jax.random.fold_in(part_splits[3], 1), PBLOCKS // PBLK)
    block_owner_turns = jax.random.permutation(jax.random.fold_in(part_splits[3], 3), PBLOCKS // PBLK)
    block_owner = jax.vmap(lambda own, number: shared_out(jax.random.fold_in(part_splits[3], 2), own, number, PBLK, N_WIDE, 1, CAP, 2))(block_owner_keys, block_owner_turns).reshape((PBLOCKS, 1))
    block_request = with_ends(jax.random.randint(part_splits[4], (PBLOCKS,), 0, REQ_DEV), jax.random.fold_in(part_splits[4], 1), 0, REQ_DEV - 1).astype(jnp.int32)
    block_admit = with_ends((jax.random.randint(part_splits[5], (PBLOCKS,), 0, 4) < 3).astype(jnp.int32), jax.random.fold_in(part_splits[5], 1), 0, 1)
    cache_kv = noise(part_splits[6], (REQUESTS, CACHE, KVW), 1.0, 6.0, ((0, 4), (2, 4)))
    cache_len = with_ends(jax.random.randint(part_splits[7], (REQUESTS,), 1, CACHE + 1), jax.random.fold_in(part_splits[7], 1), 1, CACHE).astype(jnp.int32)
    queries = draw_queries(jax.random.fold_in(jax.random.fold_in(arg_keys[10], part), 71), part)
    draft_kv = draw_draft_kv(jax.random.fold_in(jax.random.fold_in(arg_keys[10], part), 71), part)
    return dict(prompt_states=prompt_states, norm_gain=norm_gain, kv_weight=kv_weight, block_owner=block_owner, block_request=block_request, block_admit=block_admit, cache_kv=cache_kv, cache_len=cache_len, queries=queries, draft_kv=draft_kv)


def reference(prompt_states, norm_gain, kv_weight, block_owner, block_request, block_admit, cache_kv, cache_len, queries, draft_kv):
    states = prompt_states.astype(jnp.float32)
    inverse = lax.rsqrt(lax.optimization_barrier(jnp.mean(states * states, axis=1)) + 1e-05)
    scaled = (states * norm_gain).astype(jnp.bfloat16)
    slice_width = D // N_MP
    projected = jnp.zeros((PTOKENS, KVW), jnp.float32)
    for index in range(N_MP):
        lower = index * slice_width
        partial_value = jnp.dot(scaled[:, lower:lower + slice_width], kv_weight[lower:lower + slice_width], preferred_element_type=jnp.float32)
        projected = projected + partial_value.astype(jnp.bfloat16).astype(jnp.float32)
    prompt_kv = (projected * inverse[:, None]).astype(jnp.bfloat16)
    target = block_owner[:, 0] * REQ_DEV + block_request
    labels = jnp.where(block_admit == 1, target, -1).astype(jnp.int32)
    token_labels = jnp.repeat(labels, BLK)
    prompt_rows = prompt_kv.astype(jnp.float32).reshape(PTOKENS, KVH, 2, HD)
    groups = QH // KVH
    factor = 1.0 / math.sqrt(HD)
    positions = jnp.arange(CACHE, dtype=jnp.int32)
    step_index = jnp.arange(STEPS, dtype=jnp.int32)
    causal = step_index[None, :] <= step_index[:, None]

    def one_request(items):
        ident, query, cache, length, draft = items
        qvec = query.astype(jnp.float32).reshape(STEPS, KVH, groups, HD)
        cached = cache.astype(jnp.float32).reshape(CACHE, KVH, 2, HD)
        drafted = draft.astype(jnp.float32).reshape(STEPS, KVH, 2, HD)
        keys = jnp.concatenate([cached[:, :, 0], prompt_rows[:, :, 0], drafted[:, :, 0]], axis=0)
        values = jnp.concatenate([cached[:, :, 1], prompt_rows[:, :, 1], drafted[:, :, 1]], axis=0)
        cache_ok = jnp.broadcast_to((positions < length)[None, :], (STEPS, CACHE))
        prompt_ok = jnp.broadcast_to((token_labels == ident)[None, :], (STEPS, PTOKENS))
        allowed = jnp.concatenate([cache_ok, prompt_ok, causal], axis=1)[:, None, None, :]
        scores = jnp.einsum('tkgd,nkd->tkgn', qvec, keys, precision=lax.Precision.HIGHEST) * factor
        masked = jnp.where(allowed, scores, -1e+30)
        highest = lax.optimization_barrier(jnp.max(masked, axis=-1))
        weights = jnp.where(allowed, jnp.exp(masked - highest[..., None]), 0.0)
        summed = jnp.einsum('tkgn,nkd->tkgd', weights, values, precision=lax.Precision.HIGHEST)
        result = summed / lax.optimization_barrier(jnp.sum(weights, axis=-1))[..., None]
        return result.reshape(STEPS, QH * HD).astype(jnp.bfloat16)
    idents = jnp.arange(REQUESTS, dtype=jnp.int32)
    return lax.map(one_request, (idents, queries, cache_kv, cache_len, draft_kv))
```

```python
import functools
import math

import jax
import jax.numpy as jnp
from jax import lax
from jax.experimental import pallas as pl
from jax.experimental.pallas import tpu as pltpu
from jax.sharding import PartitionSpec as P

D = 8192
KVH = 8
HD = 128
QH = 64
BLK = 16
CACHE = 2048
STEPS = 4


def absorb(state, scores, allowed, values, form):
    highest, total, summed = state
    masked = jnp.where(allowed, scores, -1e30)
    new_top = jnp.maximum(highest, jnp.max(masked, axis=-1))
    weights = jnp.where(allowed, jnp.exp(masked - new_top[..., None]), 0.0)
    shrink = jnp.exp(highest - new_top)
    total = total * shrink + jnp.sum(weights, axis=-1)
    summed = summed * shrink[..., None] + jnp.einsum(
        form, weights, values.astype(jnp.float32), precision=lax.Precision.HIGHEST
    )
    return (new_top, total, summed)


def shared_keys(state, qvec, keys, values, allowed):
    scores = jnp.einsum("rskgd,nkd->rskgn", qvec, keys, preferred_element_type=jnp.float32) * (
        1.0 / math.sqrt(HD)
    )
    return absorb(state, scores, allowed[:, None, None, None, :], values, "rskgn,nkd->rskgd")


def own_keys(state, qvec, keys, values, allowed):
    scores = jnp.einsum("rskgd,rnkd->rskgn", qvec, keys, preferred_element_type=jnp.float32) * (
        1.0 / math.sqrt(HD)
    )
    return absorb(state, scores, allowed, values, "rskgn,rnkd->rskgd")


def on_device(
    prompt_states,
    norm_gain,
    kv_weight,
    block_owner,
    block_request,
    block_admit,
    cache_kv,
    cache_len,
    queries,
    draft_kv,
):
    wide = lax.axis_size("wide")
    states = prompt_states.astype(jnp.float32)
    squares = lax.psum(jnp.sum(states * states, axis=1), "mp")
    inverse = lax.rsqrt(squares / D + 1e-05)
    scaled = (states * norm_gain).astype(jnp.bfloat16)
    partial_kv = jnp.dot(
        scaled,
        lax.all_gather(kv_weight, "wide", axis=1, tiled=True),
        preferred_element_type=jnp.float32,
    )
    rounded_kv = partial_kv.astype(jnp.bfloat16).astype(jnp.float32)
    summed_kv = lax.psum_scatter(
        rounded_kv.astype(jnp.bfloat16), "mp", scatter_dimension=1, tiled=True
    ).astype(jnp.float32)
    prompt_kv = (summed_kv * inverse[:, None]).astype(jnp.bfloat16)
    width = cache_kv.shape[2]
    heads_here = width // (2 * HD)
    groups = QH // KVH
    req_dev = queries.shape[0]
    pblk = block_request.shape[0]
    blocks = prompt_kv.reshape(pblk, BLK, width)
    local_ids = jnp.arange(req_dev, dtype=jnp.int32)
    qvec = queries.reshape(req_dev, STEPS, heads_here, groups, HD)
    state = (
        jnp.full((req_dev, STEPS, heads_here, groups), -1e30, jnp.float32),
        jnp.zeros((req_dev, STEPS, heads_here, groups), jnp.float32),
        jnp.zeros((req_dev, STEPS, heads_here, groups, HD), jnp.float32),
    )
    cached = cache_kv.reshape(req_dev, CACHE, heads_here, 2, HD)
    cache_ok = (jnp.arange(CACHE, dtype=jnp.int32)[None, :] < cache_len[:, None])[
        :, None, None, None, :
    ]
    state = own_keys(state, qvec, cached[:, :, :, 0], cached[:, :, :, 1], cache_ok)
    drafted = draft_kv.reshape(req_dev, STEPS, heads_here, 2, HD)
    step_index = jnp.arange(STEPS, dtype=jnp.int32)
    causal = (step_index[None, :] <= step_index[:, None])[None, :, None, None, :]
    state = own_keys(state, qvec, drafted[:, :, :, 0], drafted[:, :, :, 1], causal)
    owner = block_owner[:, 0]
    capacity = max(2, (2 * pblk + wide - 1) // wide)
    hits = (owner[:, None] == jnp.arange(wide, dtype=jnp.int32)[None, :]).astype(jnp.int32)
    slot = jnp.sum((jnp.cumsum(hits, axis=0) - hits) * hits, axis=1)
    outgoing = jnp.zeros((wide, capacity, BLK, width), jnp.bfloat16).at[owner, slot].set(blocks)
    tagged = jnp.where(block_admit == 1, block_request, -1)
    outgoing_labels = jnp.full((wide, capacity), -1, jnp.int32).at[owner, slot].set(tagged)
    incoming, arrived = (
        lax.all_to_all(outgoing, "wide", split_axis=0, concat_axis=0, tiled=True),
        lax.all_to_all(outgoing_labels, "wide", split_axis=0, concat_axis=0, tiled=True),
    )
    rows = incoming.reshape(-1, heads_here, 2, HD)
    token_labels = jnp.repeat(arrived.reshape(-1), BLK)
    allowed = token_labels[None, :] == local_ids[:, None]
    state = shared_keys(state, qvec, rows[:, :, 0], rows[:, :, 1], allowed)
    highest, total, summed = state
    result = summed / total[..., None]
    return result.reshape(req_dev, STEPS, heads_here * groups * HD).astype(jnp.bfloat16)


LANES = 128


def fused_kernel(
    sizes,
    x_any,
    gain_ref,
    w_any,
    label_ref,
    cache_any,
    len_ref,
    q_ref,
    draft_ref,
    out_ref,
    xbuf,
    wbuf,
    part,
    gathered,
    squares_here,
    squares,
    inverse,
    kvbuf,
    cache_buf,
    q_all,
    state_cache,
    state_out,
    state_in,
    local_sem,
    own_sem,
    right_send,
    left_send,
    z_recv,
    y_send,
    y_recv,
    q_send,
    q_recv,
    sq_send,
    sq_recv,
    rs_send,
    rs_recv,
    st_send,
    st_recv,
):
    n, m_count, rounds, heads, req_dev = sizes
    w = lax.axis_index("wide")
    me = lax.axis_index("mp")
    side = lax.axis_index("parts")
    tokens, depth = xbuf.shape
    half = depth // 2
    rows = q_ref.shape[1]
    per_req = rows // req_dev
    scale = 1.0 / math.sqrt(HD)

    x_copy = pltpu.make_async_copy(x_any, xbuf, local_sem.at[0])
    x_copy.start()
    cache_copy = pltpu.make_async_copy(cache_any, cache_buf, local_sem.at[1])
    cache_copy.start()

    def lane(s):
        return pl.ds(pl.multiple_of(s * LANES, LANES), LANES)

    my_half = pl.ds(pl.multiple_of(side * half, half), half)
    other_half = pl.ds(pl.multiple_of((1 - side) * half, half), half)

    own_copies = []
    for r in range(rounds):
        own_copies.append(
            pltpu.make_async_copy(
                w_any.at[:, pl.ds(r * LANES, LANES)], wbuf.at[r, :, lane(w)], own_sem.at[r]
            )
        )
        own_copies[-1].start()

    barrier = pltpu.get_barrier_semaphore()
    for d in range(1, n):
        pl.semaphore_signal(barrier, inc=1, device_id={"wide": lax.rem(w + d, n)})
    for d in range(1, m_count):
        pl.semaphore_signal(barrier, inc=1, device_id={"mp": lax.rem(me + d, m_count)})
    pl.semaphore_signal(barrier, inc=1, device_id={"parts": 1 - side})
    pl.semaphore_wait(barrier, n - 1 + m_count - 1 + 1)

    def own_send(r, step):
        sem = right_send if step > 0 else left_send
        return pltpu.make_async_remote_copy(
            src_ref=w_any.at[my_half, pl.ds(r * LANES, LANES)],
            dst_ref=wbuf.at[r, my_half, lane(w)],
            send_sem=sem.at[r, w],
            recv_sem=z_recv.at[r, w],
            device_id={"wide": w + step},
        )

    def forward(r, s, step):
        sem = right_send if step > 0 else left_send
        return pltpu.make_async_remote_copy(
            src_ref=wbuf.at[r, my_half, lane(s)],
            dst_ref=wbuf.at[r, my_half, lane(s)],
            send_sem=sem.at[r, s],
            recv_sem=z_recv.at[r, s],
            device_id={"wide": w + step},
        )

    def across(r, s, rows_at):
        return pltpu.make_async_remote_copy(
            src_ref=wbuf.at[r, rows_at, lane(s)],
            dst_ref=wbuf.at[r, rows_at, lane(s)],
            send_sem=y_send.at[r, s],
            recv_sem=y_recv.at[r, s],
            device_id={"parts": 1 - side},
        )

    def has_next(step):
        return w < n - 1 if step > 0 else w > 0

    def has_source(d, step):
        return w >= d if step > 0 else w + d < n

    def send_own(r):
        for step in (1, -1):

            @pl.when(has_next(step))
            def _():
                own_send(r, step).start()

    def relay(r):
        for d in range(1, n):
            for step in (1, -1):

                @pl.when(has_source(d, step))
                def _():
                    s = w - d * step
                    forward(r, s, step).wait_recv()

                    @pl.when(has_next(step))
                    def _():
                        forward(r, s, step).start()

                    across(r, s, my_half).start()

    def q_copy(d):
        return pltpu.make_async_remote_copy(
            src_ref=q_ref,
            dst_ref=q_all.at[w],
            send_sem=q_send.at[d],
            recv_sem=q_recv.at[w],
            device_id={"wide": lax.rem(w + d, n)},
        )

    def q_arrival(d):
        s = lax.rem(w + d, n)
        return pltpu.make_async_remote_copy(
            src_ref=q_ref,
            dst_ref=q_all.at[s],
            send_sem=q_send.at[d],
            recv_sem=q_recv.at[s],
            device_id={"wide": s},
        )

    def sq_copy(d, at):
        return pltpu.make_async_remote_copy(
            src_ref=squares_here,
            dst_ref=squares.at[at],
            send_sem=sq_send.at[d],
            recv_sem=sq_recv.at[at],
            device_id={"mp": lax.rem(me + d, m_count)},
        )

    def rs_copy(r, d, at):
        target = lax.rem(me + d, m_count)
        return pltpu.make_async_remote_copy(
            src_ref=part.at[r, target],
            dst_ref=gathered.at[r, at],
            send_sem=rs_send.at[r, d],
            recv_sem=rs_recv.at[r, at],
            device_id={"mp": target},
        )

    def st_copy(h, d, at):
        target = lax.rem(w + d, n)
        return pltpu.make_async_remote_copy(
            src_ref=state_out.at[h, target],
            dst_ref=state_in.at[h, at],
            send_sem=st_send.at[h, d],
            recv_sem=st_recv.at[h, at],
            device_id={"wide": target},
        )

    def multiply(r):
        own_copies[r].wait()
        for d in range(1, n):
            across(r, lax.rem(w + d, n), other_half).wait_recv()
        block = min(128, tokens)

        @pl.loop(0, tokens // block)
        def _(i):
            at = pl.ds(pl.multiple_of(i * block, block), block)
            product = jnp.dot(xbuf[at, :], wbuf[r], preferred_element_type=jnp.float32)
            for m in range(m_count):
                part[r, m, at, :] = product[:, m * LANES : (m + 1) * LANES].astype(jnp.bfloat16)

        for d in range(1, m_count):
            rs_copy(r, d, me).start()

    def reduce(r):
        total = part[r, me].astype(jnp.float32)
        for d in range(1, m_count):
            s = lax.rem(me + d, m_count)
            rs_copy(r, d, s).wait_recv()
            total = total + gathered[r, s].astype(jnp.float32)
        kvbuf[r] = (total * inverse[...]).astype(jnp.bfloat16)

    def pack(out, top, total):
        at = lax.broadcasted_iota(jnp.int32, (out.shape[0], LANES), 1)
        return out, jnp.where(at < LANES // 2, top, total)

    def attend_prompt(h):
        q = q_all[:, h].reshape(n * rows, HD)
        scores = lax.dot_general(
            q, kvbuf[2 * h], (((1,), (1,)), ((), ())), preferred_element_type=jnp.float32
        ) * scale
        request = lax.broadcasted_iota(jnp.int32, (n * rows, 1), 0) // per_req
        allowed = label_ref[...] == request
        scores = jnp.where(allowed, scores, -1e30)
        top = jnp.max(scores, axis=1, keepdims=True)
        weights = jnp.where(allowed, jnp.exp(scores - top), 0.0)
        total = jnp.sum(weights, axis=1, keepdims=True)
        out = jnp.dot(
            weights.astype(jnp.bfloat16), kvbuf[2 * h + 1], preferred_element_type=jnp.float32
        )
        out, both = pack(out, top, total)
        state_out[h, :, :, :HD] = out.reshape(n, rows, HD)
        state_out[h, :, :, HD:] = both.reshape(n, rows, LANES)
        for d in range(1, n):
            st_copy(h, d, w).start()

    def attend_cache():
        step_row = lax.broadcasted_iota(jnp.int32, (per_req, 1), 0) // (per_req // STEPS)
        for a in range(req_dev):
            for h in range(heads):
                q = q_ref[h, a * per_req : (a + 1) * per_req, :]
                base = 2 * h * HD
                keys = cache_buf[a, :, base : base + HD]
                values = cache_buf[a, :, base + HD : base + 2 * HD]
                over = (((1,), (1,)), ((), ()))
                sc = lax.dot_general(q, keys, over, preferred_element_type=jnp.float32) * scale
                ok = lax.broadcasted_iota(jnp.int32, sc.shape, 1) < len_ref[a]
                sc = jnp.where(ok, sc, -1e30)
                dk = draft_ref[a, :, base : base + HD]
                dv = draft_ref[a, :, base + HD : base + 2 * HD]
                sd = lax.dot_general(q, dk, over, preferred_element_type=jnp.float32) * scale
                seen = lax.broadcasted_iota(jnp.int32, sd.shape, 1) <= step_row
                sd = jnp.where(seen, sd, -1e30)
                top = jnp.maximum(
                    jnp.max(sc, axis=1, keepdims=True), jnp.max(sd, axis=1, keepdims=True)
                )
                wc = jnp.where(ok, jnp.exp(sc - top), 0.0)
                wd = jnp.where(seen, jnp.exp(sd - top), 0.0)
                total = jnp.sum(wc, axis=1, keepdims=True) + jnp.sum(wd, axis=1, keepdims=True)
                out = jnp.dot(wc.astype(jnp.bfloat16), values, preferred_element_type=jnp.float32)
                out = out + jnp.dot(
                    wd.astype(jnp.bfloat16), dv, preferred_element_type=jnp.float32
                )
                out, both = pack(out, top, total)
                at = pl.ds(a * per_req, per_req)
                state_cache[h, at, :HD] = out
                state_cache[h, at, HD:] = both

    def merge(h):
        states = [state_cache[h], state_out[h, w]]
        for d in range(1, n):
            s = lax.rem(w + d, n)
            st_copy(h, d, s).wait_recv()
            states.append(state_in[h, s])
        tops = [state[:, HD : HD + 1] for state in states]
        top = functools.reduce(jnp.maximum, tops)
        total, out = 0.0, 0.0
        for state, its_top in zip(states, tops):
            factor = jnp.exp(its_top - top)
            total = total + factor * state[:, HD + LANES - 1 : HD + LANES]
            out = out + factor * state[:, :HD]
        out_ref[h] = (out / total).astype(out_ref.dtype)

    send_own(0)
    for d in range(1, n):
        q_copy(d).start()
    q_all[w] = q_ref[...]
    x_copy.wait()
    strip = min(64, tokens)

    @pl.loop(0, tokens // strip)
    def _(i):
        at = pl.ds(pl.multiple_of(i * strip, strip), strip)
        sums = jnp.zeros((strip, LANES), jnp.float32)
        for c in range(depth // LANES):
            cut = slice(c * LANES, (c + 1) * LANES)
            piece = xbuf[at, cut].astype(jnp.float32)
            sums = sums + piece * piece
            xbuf[at, cut] = (piece * gain_ref[:, cut]).astype(jnp.bfloat16)
        squares_here[at, :] = sums

    for d in range(1, m_count):
        sq_copy(d, me).start()

    for r in range(rounds + 2):
        if r + 1 < rounds:
            send_own(r + 1)
        if r < rounds:
            relay(r)
        if r == 0:
            cache_copy.wait()
            attend_cache()
        if r == 1:
            total = squares_here[...]
            for d in range(1, m_count):
                s = lax.rem(me + d, m_count)
                sq_copy(d, s).wait_recv()
                total = total + squares[s]
            mean = jnp.sum(total, axis=1, keepdims=True) / D
            inverse[...] = jnp.broadcast_to(lax.rsqrt(mean + 1e-05), inverse.shape)
            for d in range(1, n):
                q_arrival(d).wait_recv()
        if 1 <= r <= rounds:
            multiply(r - 1)
        if r >= 2:
            reduce(r - 2)
            if r % 2 == 1:
                attend_prompt((r - 3) // 2)
    for h in range(heads):
        merge(h)

    for r in range(rounds):
        for step in (1, -1):

            @pl.when(has_next(step))
            def _():
                own_send(r, step).wait_send()

        for d in range(1, n):
            for step in (1, -1):

                @pl.when(has_source(d, step))
                def _():
                    s = w - d * step

                    @pl.when(has_next(step))
                    def _():
                        forward(r, s, step).wait_send()

                    across(r, s, my_half).wait_send()

        for d in range(1, m_count):
            rs_copy(r, d, me).wait_send()
    for d in range(1, n):
        q_copy(d).wait_send()
        for h in range(heads):
            st_copy(h, d, w).wait_send()
    for d in range(1, m_count):
        sq_copy(d, me).wait_send()


def on_device_fused(
    mesh,
    prompt_states,
    norm_gain,
    kv_weight,
    block_owner,
    block_request,
    block_admit,
    cache_kv,
    cache_len,
    queries,
    draft_kv,
):
    n, m_count = mesh.shape["wide"], mesh.shape["mp"]
    tokens, depth = prompt_states.shape
    columns = kv_weight.shape[1]
    req_dev, cached, width = cache_kv.shape
    if mesh.shape["parts"] != 2 or n != m_count or columns % (2 * HD) or HD != LANES:
        return on_device(
            prompt_states,
            norm_gain,
            kv_weight,
            block_owner,
            block_request,
            block_admit,
            cache_kv,
            cache_len,
            queries,
            draft_kv,
        )
    rounds = columns // LANES
    heads = width // (2 * HD)
    groups = QH // KVH
    rows = req_dev * STEPS * groups
    label = jnp.where(block_admit == 1, block_owner[:, 0] * req_dev + block_request, -1)
    labels = jnp.repeat(label, BLK)[None, :]
    q = queries.reshape(req_dev, STEPS, heads, groups, HD)
    q = q.transpose(2, 0, 1, 3, 4).reshape(heads, rows, HD)
    draft = jnp.pad(draft_kv, ((0, 0), (0, 16 - STEPS), (0, 0)))
    f32, bf16 = jnp.float32, jnp.bfloat16
    vmem = pl.BlockSpec(memory_space=pltpu.VMEM)
    anywhere = pl.BlockSpec(memory_space=pl.ANY)
    dma = pltpu.SemaphoreType.DMA
    result = pl.pallas_call(
        functools.partial(fused_kernel, (n, m_count, rounds, heads, req_dev)),
        out_shape=jax.ShapeDtypeStruct((heads, rows, HD), bf16),
        in_specs=[
            anywhere,
            vmem,
            anywhere,
            vmem,
            anywhere,
            pl.BlockSpec(memory_space=pltpu.SMEM),
            vmem,
            vmem,
        ],
        out_specs=vmem,
        scratch_shapes=[
            pltpu.VMEM((tokens, depth), bf16),
            pltpu.VMEM((rounds, depth, n * LANES), bf16),
            pltpu.VMEM((rounds, m_count, tokens, LANES), bf16),
            pltpu.VMEM((rounds, m_count, tokens, LANES), bf16),
            pltpu.VMEM((tokens, LANES), f32),
            pltpu.VMEM((m_count, tokens, LANES), f32),
            pltpu.VMEM((tokens, LANES), f32),
            pltpu.VMEM((rounds, tokens, LANES), bf16),
            pltpu.VMEM((req_dev, cached, width), bf16),
            pltpu.VMEM((n, heads, rows, HD), bf16),
            pltpu.VMEM((heads, rows, 2 * LANES), f32),
            pltpu.VMEM((heads, n, rows, 2 * LANES), f32),
            pltpu.VMEM((heads, n, rows, 2 * LANES), f32),
            dma((2,)),
            dma((rounds,)),
            dma((rounds, n)),
            dma((rounds, n)),
            dma((rounds, n)),
            dma((rounds, n)),
            dma((rounds, n)),
            dma((n,)),
            dma((n,)),
            dma((m_count,)),
            dma((m_count,)),
            dma((rounds, m_count)),
            dma((rounds, m_count)),
            dma((heads, n)),
            dma((heads, n)),
        ],
        compiler_params=pltpu.CompilerParams(
            collective_id=0, has_side_effects=True, vmem_limit_bytes=60 << 20
        ),
    )(
        prompt_states,
        norm_gain[None, :],
        kv_weight,
        labels,
        cache_kv,
        cache_len,
        q,
        draft,
    )
    result = result.reshape(heads, req_dev, STEPS, groups, HD).transpose(1, 2, 0, 3, 4)
    return result.reshape(req_dev, STEPS, heads * groups * HD)


def solution(mesh):
    placed = (
        P(("parts", "wide"), "mp"),
        P("mp"),
        P("mp", "wide"),
        P(("parts", "wide"), None),
        P(("parts", "wide")),
        P(("parts", "wide")),
        P(("parts", "wide"), None, "mp"),
        P(("parts", "wide")),
        P(("parts", "wide"), None, "mp"),
        P(("parts", "wide"), None, "mp"),
    )
    return jax.shard_map(
        functools.partial(on_device_fused, mesh),
        mesh=mesh,
        in_specs=placed,
        out_specs=P(("parts", "wide"), None, "mp"),
        check_vma=False,
    )
```

```python
import functools
import math

import jax
import jax.numpy as jnp
from jax import lax
from jax.experimental import pallas as pl
from jax.experimental.pallas import tpu as pltpu
from jax.sharding import PartitionSpec as P

D = 8192
KVH = 8
HD = 128
QH = 64
BLK = 16
CACHE = 2048
STEPS = 4


def absorb(state, scores, allowed, values, form):
    highest, total, summed = state
    masked = jnp.where(allowed, scores, -1e30)
    new_top = jnp.maximum(highest, jnp.max(masked, axis=-1))
    weights = jnp.where(allowed, jnp.exp(masked - new_top[..., None]), 0.0)
    shrink = jnp.exp(highest - new_top)
    total = total * shrink + jnp.sum(weights, axis=-1)
    summed = summed * shrink[..., None] + jnp.einsum(
        form, weights, values.astype(jnp.float32), precision=lax.Precision.HIGHEST
    )
    return (new_top, total, summed)


def shared_keys(state, qvec, keys, values, allowed):
    scores = jnp.einsum("rskgd,nkd->rskgn", qvec, keys, preferred_element_type=jnp.float32) * (
        1.0 / math.sqrt(HD)
    )
    return absorb(state, scores, allowed[:, None, None, None, :], values, "rskgn,nkd->rskgd")


def own_keys(state, qvec, keys, values, allowed):
    scores = jnp.einsum("rskgd,rnkd->rskgn", qvec, keys, preferred_element_type=jnp.float32) * (
        1.0 / math.sqrt(HD)
    )
    return absorb(state, scores, allowed, values, "rskgn,rnkd->rskgd")


def on_device(
    prompt_states,
    norm_gain,
    kv_weight,
    block_owner,
    block_request,
    block_admit,
    cache_kv,
    cache_len,
    queries,
    draft_kv,
):
    wide = lax.axis_size("wide")
    states = prompt_states.astype(jnp.float32)
    squares = lax.psum(jnp.sum(states * states, axis=1), "mp")
    inverse = lax.rsqrt(squares / D + 1e-05)
    scaled = (states * norm_gain).astype(jnp.bfloat16)
    partial_kv = jnp.dot(
        scaled,
        lax.all_gather(kv_weight, "wide", axis=1, tiled=True),
        preferred_element_type=jnp.float32,
    )
    rounded_kv = partial_kv.astype(jnp.bfloat16).astype(jnp.float32)
    summed_kv = lax.psum_scatter(
        rounded_kv.astype(jnp.bfloat16), "mp", scatter_dimension=1, tiled=True
    ).astype(jnp.float32)
    prompt_kv = (summed_kv * inverse[:, None]).astype(jnp.bfloat16)
    width = cache_kv.shape[2]
    heads_here = width // (2 * HD)
    groups = QH // KVH
    req_dev = queries.shape[0]
    pblk = block_request.shape[0]
    blocks = prompt_kv.reshape(pblk, BLK, width)
    local_ids = jnp.arange(req_dev, dtype=jnp.int32)
    qvec = queries.reshape(req_dev, STEPS, heads_here, groups, HD)
    state = (
        jnp.full((req_dev, STEPS, heads_here, groups), -1e30, jnp.float32),
        jnp.zeros((req_dev, STEPS, heads_here, groups), jnp.float32),
        jnp.zeros((req_dev, STEPS, heads_here, groups, HD), jnp.float32),
    )
    cached = cache_kv.reshape(req_dev, CACHE, heads_here, 2, HD)
    cache_ok = (jnp.arange(CACHE, dtype=jnp.int32)[None, :] < cache_len[:, None])[
        :, None, None, None, :
    ]
    state = own_keys(state, qvec, cached[:, :, :, 0], cached[:, :, :, 1], cache_ok)
    drafted = draft_kv.reshape(req_dev, STEPS, heads_here, 2, HD)
    step_index = jnp.arange(STEPS, dtype=jnp.int32)
    causal = (step_index[None, :] <= step_index[:, None])[None, :, None, None, :]
    state = own_keys(state, qvec, drafted[:, :, :, 0], drafted[:, :, :, 1], causal)
    owner = block_owner[:, 0]
    capacity = max(2, (2 * pblk + wide - 1) // wide)
    hits = (owner[:, None] == jnp.arange(wide, dtype=jnp.int32)[None, :]).astype(jnp.int32)
    slot = jnp.sum((jnp.cumsum(hits, axis=0) - hits) * hits, axis=1)
    outgoing = jnp.zeros((wide, capacity, BLK, width), jnp.bfloat16).at[owner, slot].set(blocks)
    tagged = jnp.where(block_admit == 1, block_request, -1)
    outgoing_labels = jnp.full((wide, capacity), -1, jnp.int32).at[owner, slot].set(tagged)
    incoming, arrived = (
        lax.all_to_all(outgoing, "wide", split_axis=0, concat_axis=0, tiled=True),
        lax.all_to_all(outgoing_labels, "wide", split_axis=0, concat_axis=0, tiled=True),
    )
    rows = incoming.reshape(-1, heads_here, 2, HD)
    token_labels = jnp.repeat(arrived.reshape(-1), BLK)
    allowed = token_labels[None, :] == local_ids[:, None]
    state = shared_keys(state, qvec, rows[:, :, 0], rows[:, :, 1], allowed)
    highest, total, summed = state
    result = summed / total[..., None]
    return result.reshape(req_dev, STEPS, heads_here * groups * HD).astype(jnp.bfloat16)


LANES = 128


def fused_kernel(
    sizes,
    x_any,
    gain_ref,
    w_any,
    owner_ref,
    request_ref,
    admit_ref,
    cache_any,
    len_ref,
    query_ref,
    draft_ref,
    out_ref,
    xbuf,
    wbuf,
    part,
    gathered,
    squares_here,
    squares,
    inverse,
    kvbuf,
    cache_buf,
    q_here,
    q_all,
    labels,
    prob,
    cache_out,
    cache_ml,
    out_send,
    out_recv,
    ml_send,
    ml_recv,
    local_sem,
    own_sem,
    right_send,
    left_send,
    z_recv,
    y_send,
    y_recv,
    q_send,
    q_recv,
    sq_send,
    sq_recv,
    rs_send,
    rs_recv,
    st_send,
    st_recv,
    mls_send,
    mls_recv,
):
    n, m_count, rounds, heads, req_dev, pieces = sizes
    w = lax.axis_index("wide")
    me = lax.axis_index("mp")
    side = lax.axis_index("parts")
    tokens, depth = xbuf.shape
    half = depth // 2
    rows = q_here.shape[1]
    groups = rows // (req_dev * STEPS)
    piece = half // pieces
    per_req = rows // req_dev
    scale = 1.0 / math.sqrt(HD)

    x_copy = pltpu.make_async_copy(x_any, xbuf, local_sem.at[0])
    x_copy.start()
    cache_copy = pltpu.make_async_copy(cache_any, cache_buf, local_sem.at[1])
    cache_copy.start()

    def lane(s):
        return pl.ds(pl.multiple_of(s * LANES, LANES), LANES)

    def rows_of(whose, k):
        return pl.ds(pl.multiple_of(whose * half + k * piece, piece), piece)

    own_copies = []
    for r in range(rounds):
        own_copies.append(
            pltpu.make_async_copy(
                w_any.at[:, pl.ds(r * LANES, LANES)], wbuf.at[r, :, lane(w)], own_sem.at[r]
            )
        )
        own_copies[-1].start()

    barrier = pltpu.get_barrier_semaphore()
    for d in range(1, n):
        pl.semaphore_signal(barrier, inc=1, device_id={"wide": lax.rem(w + d, n)})
    for d in range(1, m_count):
        pl.semaphore_signal(barrier, inc=1, device_id={"mp": lax.rem(me + d, m_count)})
    pl.semaphore_signal(barrier, inc=1, device_id={"parts": 1 - side})
    pl.semaphore_wait(barrier, n - 1 + m_count - 1 + 1)

    def own_send(r, k, step):
        sem = right_send if step > 0 else left_send
        return pltpu.make_async_remote_copy(
            src_ref=w_any.at[rows_of(side, k), pl.ds(r * LANES, LANES)],
            dst_ref=wbuf.at[r, rows_of(side, k), lane(w)],
            send_sem=sem.at[r * pieces + k, w],
            recv_sem=z_recv.at[r * pieces + k, w],
            device_id={"wide": w + step},
        )

    def forward(r, k, s, step):
        sem = right_send if step > 0 else left_send
        return pltpu.make_async_remote_copy(
            src_ref=wbuf.at[r, rows_of(side, k), lane(s)],
            dst_ref=wbuf.at[r, rows_of(side, k), lane(s)],
            send_sem=sem.at[r * pieces + k, s],
            recv_sem=z_recv.at[r * pieces + k, s],
            device_id={"wide": w + step},
        )

    def across(r, k, s, whose):
        return pltpu.make_async_remote_copy(
            src_ref=wbuf.at[r, rows_of(whose, k), lane(s)],
            dst_ref=wbuf.at[r, rows_of(whose, k), lane(s)],
            send_sem=y_send.at[r * pieces + k, s],
            recv_sem=y_recv.at[r * pieces + k, s],
            device_id={"parts": 1 - side},
        )

    def has_next(step):
        return w < n - 1 if step > 0 else w > 0

    def has_source(d, step):
        return w >= d if step > 0 else w + d < n

    def send_own(r, k):
        for step in (1, -1):

            @pl.when(has_next(step))
            def _():
                own_send(r, k, step).start()

    def relay(r, k):
        for d in range(1, n):
            for step in (1, -1):

                @pl.when(has_source(d, step))
                def _():
                    s = w - d * step
                    forward(r, k, s, step).wait_recv()

                    @pl.when(has_next(step))
                    def _():
                        forward(r, k, s, step).start()

                    across(r, k, s, side).start()

    def q_copy(d):
        return pltpu.make_async_remote_copy(
            src_ref=q_here,
            dst_ref=q_all.at[w],
            send_sem=q_send.at[d],
            recv_sem=q_recv.at[w],
            device_id={"wide": lax.rem(w + d, n)},
        )

    def q_arrival(d):
        s = lax.rem(w + d, n)
        return pltpu.make_async_remote_copy(
            src_ref=q_here,
            dst_ref=q_all.at[s],
            send_sem=q_send.at[d],
            recv_sem=q_recv.at[s],
            device_id={"wide": s},
        )

    def sq_copy(d, at):
        return pltpu.make_async_remote_copy(
            src_ref=squares_here,
            dst_ref=squares.at[at],
            send_sem=sq_send.at[d],
            recv_sem=sq_recv.at[at],
            device_id={"mp": lax.rem(me + d, m_count)},
        )

    def rs_copy(r, d, at):
        target = lax.rem(me + d, m_count)
        return pltpu.make_async_remote_copy(
            src_ref=part.at[r, target],
            dst_ref=gathered.at[r, at],
            send_sem=rs_send.at[r, d],
            recv_sem=rs_recv.at[r, at],
            device_id={"mp": target},
        )

    def state_copy(h, d, at, values):
        target = lax.rem(w + d, n)
        source, sink = (out_send, out_recv) if values else (ml_send, ml_recv)
        gone, come = (st_send, st_recv) if values else (mls_send, mls_recv)
        return pltpu.make_async_remote_copy(
            src_ref=source.at[h, target],
            dst_ref=sink.at[h, at],
            send_sem=gone.at[h, d],
            recv_sem=come.at[h, at],
            device_id={"wide": target},
        )

    def multiply(r):
        own_copies[r].wait()
        for k in range(pieces):
            for d in range(1, n):
                across(r, k, lax.rem(w + d, n), 1 - side).wait_recv()
        block = min(128, tokens)

        @pl.loop(0, tokens // block)
        def _(i):
            at = pl.ds(pl.multiple_of(i * block, block), block)
            product = jnp.dot(xbuf[at, :], wbuf[r], preferred_element_type=jnp.float32)
            for m in range(m_count):
                part[r, m, at, :] = product[:, m * LANES : (m + 1) * LANES].astype(jnp.bfloat16)

        for d in range(1, m_count):
            rs_copy(r, d, me).start()

    def reduce(r):
        total = part[r, me].astype(jnp.float32)
        for d in range(1, m_count):
            s = lax.rem(me + d, m_count)
            rs_copy(r, d, s).wait_recv()
            total = total + gathered[r, s].astype(jnp.float32)
        kvbuf[r] = (total * inverse[...]).astype(jnp.bfloat16)

    def pack(top, total):
        at = lax.broadcasted_iota(jnp.int32, (top.shape[0], LANES), 1)
        return jnp.where(at < LANES // 2, top, total)

    def attend_scores(h):
        q = q_all[:, h].reshape(n * rows, HD)
        scores = lax.dot_general(
            q, kvbuf[2 * h], (((1,), (1,)), ((), ())), preferred_element_type=jnp.float32
        ) * scale
        request = lax.broadcasted_iota(jnp.int32, (n * rows, 1), 0) // per_req
        allowed = labels[0:1, :] == request
        scores = jnp.where(allowed, scores, -1e30)
        top = jnp.max(scores, axis=1, keepdims=True)
        weights = jnp.where(allowed, jnp.exp(scores - top), 0.0)
        total = jnp.sum(weights, axis=1, keepdims=True)
        prob[h] = weights.astype(jnp.bfloat16)
        ml_send[h] = pack(top, total).reshape(n, rows, LANES)
        for d in range(1, n):
            state_copy(h, d, w, False).start()

    def attend_values(h):
        out = jnp.dot(prob[h], kvbuf[2 * h + 1], preferred_element_type=jnp.float32)
        out_send[h] = out.astype(jnp.bfloat16).reshape(n, rows, HD)
        for d in range(1, n):
            state_copy(h, d, w, True).start()

    def attend_cache(a):
        step_row = lax.rem(lax.broadcasted_iota(jnp.int32, (per_req, 1), 0), STEPS)
        drafted = draft_ref[a].astype(jnp.float32)
        drafted = jnp.concatenate(
            [drafted, jnp.zeros((16 - STEPS, drafted.shape[1]), jnp.float32)], axis=0
        ).astype(jnp.bfloat16)
        for h in range(heads):
            q = q_here[h, a * per_req : (a + 1) * per_req, :]
            base = 2 * h * HD
            keys = cache_buf[a, :, base : base + HD]
            values = cache_buf[a, :, base + HD : base + 2 * HD]
            over = (((1,), (1,)), ((), ()))
            sc = lax.dot_general(q, keys, over, preferred_element_type=jnp.float32) * scale
            ok = lax.broadcasted_iota(jnp.int32, sc.shape, 1) < len_ref[a]
            sc = jnp.where(ok, sc, -1e30)
            dk = drafted[:, base : base + HD]
            dv = drafted[:, base + HD : base + 2 * HD]
            sd = lax.dot_general(q, dk, over, preferred_element_type=jnp.float32) * scale
            seen = lax.broadcasted_iota(jnp.int32, sd.shape, 1) <= step_row
            sd = jnp.where(seen, sd, -1e30)
            top = jnp.maximum(
                jnp.max(sc, axis=1, keepdims=True), jnp.max(sd, axis=1, keepdims=True)
            )
            wc = jnp.where(ok, jnp.exp(sc - top), 0.0)
            wd = jnp.where(seen, jnp.exp(sd - top), 0.0)
            total = jnp.sum(wc, axis=1, keepdims=True) + jnp.sum(wd, axis=1, keepdims=True)
            out = jnp.dot(wc.astype(jnp.bfloat16), values, preferred_element_type=jnp.float32)
            out = out + jnp.dot(wd.astype(jnp.bfloat16), dv, preferred_element_type=jnp.float32)
            at = pl.ds(a * per_req, per_req)
            cache_out[h, at, :] = out
            cache_ml[h, at, :] = pack(top, total)

    def factors(h):
        stats = [cache_ml[h], ml_send[h, w]]
        for d in range(1, n):
            s = lax.rem(w + d, n)
            state_copy(h, d, s, False).wait_recv()
            stats.append(ml_recv[h, s])
        tops = [each[:, 0:1] for each in stats]
        top = functools.reduce(jnp.maximum, tops)
        scaled = [jnp.exp(each - top) for each in tops]
        total = sum(f * each[:, LANES - 1 : LANES] for f, each in zip(scaled, stats))
        return [f / total for f in scaled]

    def merge(h, share):
        out = share[0] * cache_out[h] + share[1] * out_send[h, w].astype(jnp.float32)
        for d in range(1, n):
            s = lax.rem(w + d, n)
            state_copy(h, d, s, True).wait_recv()
            out = out + share[d + 1] * out_recv[h, s].astype(jnp.float32)
        for a in range(req_dev):
            for g in range(groups):
                at = (a * groups + g) * STEPS
                cut = slice((h * groups + g) * HD, (h * groups + g + 1) * HD)
                out_ref[a, :, cut] = out[at : at + STEPS, :].astype(out_ref.dtype)

    send_own(0, 0)
    for h in range(heads):
        q_here[h] = jnp.concatenate(
            [
                query_ref[a, :, (h * groups + g) * HD : (h * groups + g + 1) * HD].astype(
                    jnp.float32
                )
                for a in range(req_dev)
                for g in range(groups)
            ],
            axis=0,
        ).astype(jnp.bfloat16)
    for d in range(1, n):
        q_copy(d).start()
    q_all[w] = q_here[...]
    blocks = owner_ref.shape[0]
    shape = (blocks, blocks)
    same = lax.broadcasted_iota(jnp.int32, shape, 0) == lax.broadcasted_iota(jnp.int32, shape, 1)
    request = jnp.sum(jnp.where(same, request_ref[...], 0), axis=1, keepdims=True)
    admit = jnp.sum(jnp.where(same, admit_ref[...], 0), axis=1, keepdims=True)
    label = jnp.where(admit == 1, owner_ref[...] * req_dev + request, -1)
    shape = (blocks, tokens)
    block_of = lax.broadcasted_iota(jnp.int32, shape, 1) // (tokens // blocks)
    inside = block_of == lax.broadcasted_iota(jnp.int32, shape, 0)
    row = jnp.sum(jnp.where(inside, label, 0), axis=0, keepdims=True)
    labels[...] = jnp.broadcast_to(row, labels.shape)
    x_copy.wait()
    strip = min(64, tokens)

    @pl.loop(0, tokens // strip)
    def _(i):
        at = pl.ds(pl.multiple_of(i * strip, strip), strip)
        sums = jnp.zeros((strip, LANES), jnp.float32)
        for c in range(depth // LANES):
            cut = slice(c * LANES, (c + 1) * LANES)
            piece = xbuf[at, cut].astype(jnp.float32)
            sums = sums + piece * piece
            xbuf[at, cut] = (piece * gain_ref[:, cut]).astype(jnp.bfloat16)
        squares_here[at, :] = sums

    for d in range(1, m_count):
        sq_copy(d, me).start()

    order = [(r, k) for r in range(rounds) for k in range(pieces)]

    def stats():
        total = squares_here[...]
        for d in range(1, m_count):
            s = lax.rem(me + d, m_count)
            sq_copy(d, s).wait_recv()
            total = total + squares[s]
        mean = jnp.sum(total, axis=1, keepdims=True) / D
        inverse[...] = jnp.broadcast_to(lax.rsqrt(mean + 1e-05), inverse.shape)
        for d in range(1, n):
            q_arrival(d).wait_recv()

    def collect(r):
        reduce(r)
        if r % 2 == 0:
            attend_scores(r // 2)
        else:
            attend_values(r // 2)

    work = {}

    def plan(r, k, job):
        work.setdefault((r, min(k, pieces - 1)), []).append(job)

    for a in range(req_dev):
        plan(0, a, functools.partial(attend_cache, a))
    for r in range(1, rounds):
        plan(r, 0, functools.partial(multiply, r - 1))
        if r == 1:
            plan(r, 0, stats)
        else:
            plan(r, 1, functools.partial(collect, r - 2))
    cache_copy.wait()
    for i, (r, k) in enumerate(order):
        if i + 1 < len(order):
            send_own(*order[i + 1])
        relay(r, k)
        for job in work.get((r, k), []):
            job()
    multiply(rounds - 1)
    for r in range(max(rounds - 2, 0), rounds):
        collect(r)
    shares = [factors(h) for h in range(heads)]
    for h in range(heads):
        merge(h, shares[h])

    for r, k in order:
        for step in (1, -1):

            @pl.when(has_next(step))
            def _():
                own_send(r, k, step).wait_send()

        for d in range(1, n):
            for step in (1, -1):

                @pl.when(has_source(d, step))
                def _():
                    s = w - d * step

                    @pl.when(has_next(step))
                    def _():
                        forward(r, k, s, step).wait_send()

                    across(r, k, s, side).wait_send()

    for r in range(rounds):
        for d in range(1, m_count):
            rs_copy(r, d, me).wait_send()
    for d in range(1, n):
        q_copy(d).wait_send()
        for h in range(heads):
            state_copy(h, d, w, False).wait_send()
            state_copy(h, d, w, True).wait_send()
    for d in range(1, m_count):
        sq_copy(d, me).wait_send()


def on_device_fused(
    mesh,
    prompt_states,
    norm_gain,
    kv_weight,
    block_owner,
    block_request,
    block_admit,
    cache_kv,
    cache_len,
    queries,
    draft_kv,
):
    n, m_count = mesh.shape["wide"], mesh.shape["mp"]
    tokens, depth = prompt_states.shape
    columns = kv_weight.shape[1]
    req_dev, cached, width = cache_kv.shape
    if mesh.shape["parts"] != 2 or n != m_count or columns % (2 * HD) or HD != LANES:
        return on_device(
            prompt_states,
            norm_gain,
            kv_weight,
            block_owner,
            block_request,
            block_admit,
            cache_kv,
            cache_len,
            queries,
            draft_kv,
        )
    rounds = columns // LANES
    heads = width // (2 * HD)
    groups = QH // KVH
    rows = req_dev * STEPS * groups
    pieces = 2
    f32, bf16 = jnp.float32, jnp.bfloat16
    vmem = pl.BlockSpec(memory_space=pltpu.VMEM)
    anywhere = pl.BlockSpec(memory_space=pl.ANY)
    dma = pltpu.SemaphoreType.DMA
    return pl.pallas_call(
        functools.partial(fused_kernel, (n, m_count, rounds, heads, req_dev, pieces)),
        out_shape=jax.ShapeDtypeStruct(queries.shape, bf16),
        in_specs=[
            anywhere,
            vmem,
            anywhere,
            vmem,
            vmem,
            vmem,
            anywhere,
            pl.BlockSpec(memory_space=pltpu.SMEM),
            vmem,
            vmem,
        ],
        out_specs=vmem,
        scratch_shapes=[
            pltpu.VMEM((tokens, depth), bf16),
            pltpu.VMEM((rounds, depth, n * LANES), bf16),
            pltpu.VMEM((rounds, m_count, tokens, LANES), bf16),
            pltpu.VMEM((rounds, m_count, tokens, LANES), bf16),
            pltpu.VMEM((tokens, LANES), f32),
            pltpu.VMEM((m_count, tokens, LANES), f32),
            pltpu.VMEM((tokens, LANES), f32),
            pltpu.VMEM((rounds, tokens, LANES), bf16),
            pltpu.VMEM((req_dev, cached, width), bf16),
            pltpu.VMEM((heads, rows, HD), bf16),
            pltpu.VMEM((n, heads, rows, HD), bf16),
            pltpu.VMEM((8, tokens), jnp.int32),
            pltpu.VMEM((heads, n * rows, tokens), bf16),
            pltpu.VMEM((heads, rows, HD), f32),
            pltpu.VMEM((heads, rows, LANES), f32),
            pltpu.VMEM((heads, n, rows, HD), bf16),
            pltpu.VMEM((heads, n, rows, HD), bf16),
            pltpu.VMEM((heads, n, rows, LANES), f32),
            pltpu.VMEM((heads, n, rows, LANES), f32),
            dma((2,)),
            dma((rounds,)),
            dma((rounds * pieces, n)),
            dma((rounds * pieces, n)),
            dma((rounds * pieces, n)),
            dma((rounds * pieces, n)),
            dma((rounds * pieces, n)),
            dma((n,)),
            dma((n,)),
            dma((m_count,)),
            dma((m_count,)),
            dma((rounds, m_count)),
            dma((rounds, m_count)),
            dma((heads, n)),
            dma((heads, n)),
            dma((heads, n)),
            dma((heads, n)),
        ],
        compiler_params=pltpu.CompilerParams(
            collective_id=0, has_side_effects=True, vmem_limit_bytes=60 << 20
        ),
    )(
        prompt_states,
        norm_gain[None, :],
        kv_weight,
        block_owner,
        block_request[None, :],
        block_admit[None, :],
        cache_kv,
        cache_len,
        queries,
        draft_kv,
    )


def solution(mesh):
    placed = (
        P(("parts", "wide"), "mp"),
        P("mp"),
        P("mp", "wide"),
        P(("parts", "wide"), None),
        P(("parts", "wide")),
        P(("parts", "wide")),
        P(("parts", "wide"), None, "mp"),
        P(("parts", "wide")),
        P(("parts", "wide"), None, "mp"),
        P(("parts", "wide"), None, "mp"),
    )
    return jax.shard_map(
        functools.partial(on_device_fused, mesh),
        mesh=mesh,
        in_specs=placed,
        out_specs=P(("parts", "wide"), None, "mp"),
        check_vma=False,
    )
```

```python
import functools
import math

import jax
import jax.numpy as jnp
from jax import lax
from jax.experimental import pallas as pl
from jax.experimental.pallas import tpu as pltpu
from jax.sharding import PartitionSpec as P

D = 8192
KVH = 8
HD = 128
QH = 64
BLK = 16
CACHE = 2048
STEPS = 4


def absorb(state, scores, allowed, values, form):
    highest, total, summed = state
    masked = jnp.where(allowed, scores, -1e30)
    new_top = jnp.maximum(highest, jnp.max(masked, axis=-1))
    weights = jnp.where(allowed, jnp.exp(masked - new_top[..., None]), 0.0)
    shrink = jnp.exp(highest - new_top)
    total = total * shrink + jnp.sum(weights, axis=-1)
    summed = summed * shrink[..., None] + jnp.einsum(
        form, weights, values.astype(jnp.float32), precision=lax.Precision.HIGHEST
    )
    return (new_top, total, summed)


def shared_keys(state, qvec, keys, values, allowed):
    scores = jnp.einsum("rskgd,nkd->rskgn", qvec, keys, preferred_element_type=jnp.float32) * (
        1.0 / math.sqrt(HD)
    )
    return absorb(state, scores, allowed[:, None, None, None, :], values, "rskgn,nkd->rskgd")


def own_keys(state, qvec, keys, values, allowed):
    scores = jnp.einsum("rskgd,rnkd->rskgn", qvec, keys, preferred_element_type=jnp.float32) * (
        1.0 / math.sqrt(HD)
    )
    return absorb(state, scores, allowed, values, "rskgn,rnkd->rskgd")


def on_device(
    prompt_states,
    norm_gain,
    kv_weight,
    block_owner,
    block_request,
    block_admit,
    cache_kv,
    cache_len,
    queries,
    draft_kv,
):
    wide = lax.axis_size("wide")
    states = prompt_states.astype(jnp.float32)
    squares = lax.psum(jnp.sum(states * states, axis=1), "mp")
    inverse = lax.rsqrt(squares / D + 1e-05)
    scaled = (states * norm_gain).astype(jnp.bfloat16)
    partial_kv = jnp.dot(
        scaled,
        lax.all_gather(kv_weight, "wide", axis=1, tiled=True),
        preferred_element_type=jnp.float32,
    )
    rounded_kv = partial_kv.astype(jnp.bfloat16).astype(jnp.float32)
    summed_kv = lax.psum_scatter(
        rounded_kv.astype(jnp.bfloat16), "mp", scatter_dimension=1, tiled=True
    ).astype(jnp.float32)
    prompt_kv = (summed_kv * inverse[:, None]).astype(jnp.bfloat16)
    width = cache_kv.shape[2]
    heads_here = width // (2 * HD)
    groups = QH // KVH
    req_dev = queries.shape[0]
    pblk = block_request.shape[0]
    blocks = prompt_kv.reshape(pblk, BLK, width)
    local_ids = jnp.arange(req_dev, dtype=jnp.int32)
    qvec = queries.reshape(req_dev, STEPS, heads_here, groups, HD)
    state = (
        jnp.full((req_dev, STEPS, heads_here, groups), -1e30, jnp.float32),
        jnp.zeros((req_dev, STEPS, heads_here, groups), jnp.float32),
        jnp.zeros((req_dev, STEPS, heads_here, groups, HD), jnp.float32),
    )
    cached = cache_kv.reshape(req_dev, CACHE, heads_here, 2, HD)
    cache_ok = (jnp.arange(CACHE, dtype=jnp.int32)[None, :] < cache_len[:, None])[
        :, None, None, None, :
    ]
    state = own_keys(state, qvec, cached[:, :, :, 0], cached[:, :, :, 1], cache_ok)
    drafted = draft_kv.reshape(req_dev, STEPS, heads_here, 2, HD)
    step_index = jnp.arange(STEPS, dtype=jnp.int32)
    causal = (step_index[None, :] <= step_index[:, None])[None, :, None, None, :]
    state = own_keys(state, qvec, drafted[:, :, :, 0], drafted[:, :, :, 1], causal)
    owner = block_owner[:, 0]
    capacity = max(2, (2 * pblk + wide - 1) // wide)
    hits = (owner[:, None] == jnp.arange(wide, dtype=jnp.int32)[None, :]).astype(jnp.int32)
    slot = jnp.sum((jnp.cumsum(hits, axis=0) - hits) * hits, axis=1)
    outgoing = jnp.zeros((wide, capacity, BLK, width), jnp.bfloat16).at[owner, slot].set(blocks)
    tagged = jnp.where(block_admit == 1, block_request, -1)
    outgoing_labels = jnp.full((wide, capacity), -1, jnp.int32).at[owner, slot].set(tagged)
    incoming, arrived = (
        lax.all_to_all(outgoing, "wide", split_axis=0, concat_axis=0, tiled=True),
        lax.all_to_all(outgoing_labels, "wide", split_axis=0, concat_axis=0, tiled=True),
    )
    rows = incoming.reshape(-1, heads_here, 2, HD)
    token_labels = jnp.repeat(arrived.reshape(-1), BLK)
    allowed = token_labels[None, :] == local_ids[:, None]
    state = shared_keys(state, qvec, rows[:, :, 0], rows[:, :, 1], allowed)
    highest, total, summed = state
    result = summed / total[..., None]
    return result.reshape(req_dev, STEPS, heads_here * groups * HD).astype(jnp.bfloat16)


LANES = 128


def fused_kernel(
    sizes,
    x_any,
    gain_ref,
    w_any,
    owner_ref,
    request_ref,
    admit_ref,
    cache_any,
    len_ref,
    query_ref,
    draft_ref,
    out_ref,
    xbuf,
    wbuf,
    part,
    gathered,
    squares_here,
    squares,
    inverse,
    kvbuf,
    cache_buf,
    q_here,
    q_all,
    labels,
    prob,
    cache_out,
    cache_ml,
    out_send,
    out_recv,
    ml_send,
    ml_recv,
    local_sem,
    own_sem,
    right_send,
    left_send,
    z_recv,
    y_send,
    y_recv,
    q_send,
    q_recv,
    sq_send,
    sq_recv,
    rs_send,
    rs_recv,
    st_send,
    st_recv,
    mls_send,
    mls_recv,
):
    n, m_count, rounds, heads, req_dev, pieces = sizes
    w = lax.axis_index("wide")
    me = lax.axis_index("mp")
    side = lax.axis_index("parts")
    tokens, depth = xbuf.shape
    half = depth // 2
    rows = q_here.shape[1]
    groups = rows // (req_dev * STEPS)
    piece = half // pieces
    per_req = rows // req_dev
    scale = 1.0 / math.sqrt(HD)

    x_copy = pltpu.make_async_copy(x_any, xbuf, local_sem.at[0])
    x_copy.start()
    cache_copy = pltpu.make_async_copy(cache_any, cache_buf, local_sem.at[1])
    cache_copy.start()

    def lane(s):
        return pl.ds(pl.multiple_of(s * LANES, LANES), LANES)

    def rows_of(whose, k):
        return pl.ds(pl.multiple_of(whose * half + k * piece, piece), piece)

    own_copies = []
    for r in range(rounds):
        own_copies.append(
            pltpu.make_async_copy(
                w_any.at[:, pl.ds(r * LANES, LANES)], wbuf.at[r, :, lane(w)], own_sem.at[r]
            )
        )
        own_copies[-1].start()

    barrier = pltpu.get_barrier_semaphore()
    for d in range(1, n):
        pl.semaphore_signal(barrier, inc=1, device_id={"wide": lax.rem(w + d, n)})
    for d in range(1, m_count):
        pl.semaphore_signal(barrier, inc=1, device_id={"mp": lax.rem(me + d, m_count)})
    pl.semaphore_signal(barrier, inc=1, device_id={"parts": 1 - side})
    pl.semaphore_wait(barrier, n - 1 + m_count - 1 + 1)

    def own_send(r, k, step):
        sem = right_send if step > 0 else left_send
        return pltpu.make_async_remote_copy(
            src_ref=w_any.at[rows_of(side, k), pl.ds(r * LANES, LANES)],
            dst_ref=wbuf.at[r, rows_of(side, k), lane(w)],
            send_sem=sem.at[r * pieces + k, w],
            recv_sem=z_recv.at[r * pieces + k, w],
            device_id={"wide": w + step},
        )

    def forward(r, k, s, step):
        sem = right_send if step > 0 else left_send
        return pltpu.make_async_remote_copy(
            src_ref=wbuf.at[r, rows_of(side, k), lane(s)],
            dst_ref=wbuf.at[r, rows_of(side, k), lane(s)],
            send_sem=sem.at[r * pieces + k, s],
            recv_sem=z_recv.at[r * pieces + k, s],
            device_id={"wide": w + step},
        )

    def across(r, k, s, whose):
        return pltpu.make_async_remote_copy(
            src_ref=wbuf.at[r, rows_of(whose, k), lane(s)],
            dst_ref=wbuf.at[r, rows_of(whose, k), lane(s)],
            send_sem=y_send.at[r * pieces + k, s],
            recv_sem=y_recv.at[r * pieces + k, s],
            device_id={"parts": 1 - side},
        )

    def has_next(step):
        return w < n - 1 if step > 0 else w > 0

    def has_source(d, step):
        return w >= d if step > 0 else w + d < n

    def send_own(r, k):
        for step in (1, -1):

            @pl.when(has_next(step))
            def _():
                own_send(r, k, step).start()

    def relay(r, k):
        for d in range(1, n):
            for step in (1, -1):

                @pl.when(has_source(d, step))
                def _():
                    s = w - d * step
                    forward(r, k, s, step).wait_recv()

                    @pl.when(has_next(step))
                    def _():
                        forward(r, k, s, step).start()

                    across(r, k, s, side).start()

    def q_copy(d):
        return pltpu.make_async_remote_copy(
            src_ref=q_here,
            dst_ref=q_all.at[w],
            send_sem=q_send.at[d],
            recv_sem=q_recv.at[w],
            device_id={"wide": lax.rem(w + d, n)},
        )

    def q_arrival(d):
        s = lax.rem(w + d, n)
        return pltpu.make_async_remote_copy(
            src_ref=q_here,
            dst_ref=q_all.at[s],
            send_sem=q_send.at[d],
            recv_sem=q_recv.at[s],
            device_id={"wide": s},
        )

    def sq_copy(d, at):
        return pltpu.make_async_remote_copy(
            src_ref=squares_here,
            dst_ref=squares.at[at],
            send_sem=sq_send.at[d],
            recv_sem=sq_recv.at[at],
            device_id={"mp": lax.rem(me + d, m_count)},
        )

    def rs_copy(r, d, at):
        target = lax.rem(me + d, m_count)
        return pltpu.make_async_remote_copy(
            src_ref=part.at[r, target],
            dst_ref=gathered.at[r, at],
            send_sem=rs_send.at[r, d],
            recv_sem=rs_recv.at[r, at],
            device_id={"mp": target},
        )

    def state_copy(h, d, at, values):
        target = lax.rem(w + d, n)
        source, sink = (out_send, out_recv) if values else (ml_send, ml_recv)
        gone, come = (st_send, st_recv) if values else (mls_send, mls_recv)
        return pltpu.make_async_remote_copy(
            src_ref=source.at[h, target],
            dst_ref=sink.at[h, at],
            send_sem=gone.at[h, d],
            recv_sem=come.at[h, at],
            device_id={"wide": target},
        )

    def multiply(r):
        own_copies[r].wait()
        for k in range(pieces):
            for d in range(1, n):
                across(r, k, lax.rem(w + d, n), 1 - side).wait_recv()
        block = min(128, tokens)

        @pl.loop(0, tokens // block)
        def _(i):
            at = pl.ds(pl.multiple_of(i * block, block), block)
            product = jnp.dot(xbuf[at, :], wbuf[r], preferred_element_type=jnp.float32)
            for m in range(m_count):
                part[r, m, at, :] = product[:, m * LANES : (m + 1) * LANES].astype(jnp.bfloat16)

        for d in (*range(2, m_count), 1):
            rs_copy(r, d, me).start()

    def reduce(r):
        total = part[r, me].astype(jnp.float32)
        for d in range(1, m_count):
            s = lax.rem(me + d, m_count)
            rs_copy(r, d, s).wait_recv()
            total = total + gathered[r, s].astype(jnp.float32)
        kvbuf[r] = (total * inverse[...]).astype(jnp.bfloat16)

    def pack(top, total):
        at = lax.broadcasted_iota(jnp.int32, (top.shape[0], LANES), 1)
        return jnp.where(at < LANES // 2, top, total)

    def attend_scores(h):
        q = q_all[:, h].reshape(n * rows, HD)
        scores = lax.dot_general(
            q, kvbuf[2 * h], (((1,), (1,)), ((), ())), preferred_element_type=jnp.float32
        ) * scale
        request = lax.broadcasted_iota(jnp.int32, (n * rows, 1), 0) // per_req
        allowed = labels[0:1, :] == request
        scores = jnp.where(allowed, scores, -1e30)
        top = jnp.max(scores, axis=1, keepdims=True)
        weights = jnp.where(allowed, jnp.exp(scores - top), 0.0)
        total = jnp.sum(weights, axis=1, keepdims=True)
        prob[h] = weights.astype(jnp.bfloat16)
        both = pack(top, total)
        at = lax.broadcasted_iota(jnp.int32, both.shape, 1)
        mine = lax.rem(lax.broadcasted_iota(jnp.int32, both.shape, 0), rows)
        both = jnp.where(lax.rem(at, LANES // 2) == mine, both, 0.0)
        for o in range(n):
            row = jnp.sum(both[o * rows : (o + 1) * rows], axis=0, keepdims=True)
            ml_send[h, o] = jnp.broadcast_to(row, ml_send.shape[2:])
        for d in range(1, n):
            state_copy(h, d, w, False).start()

    def attend_values(h):
        out = jnp.dot(prob[h], kvbuf[2 * h + 1], preferred_element_type=jnp.float32)
        out_send[h] = out.astype(jnp.bfloat16).reshape(n, rows, HD)
        for d in range(1, n):
            state_copy(h, d, w, True).start()

    def attend_cache(a):
        step_row = lax.rem(lax.broadcasted_iota(jnp.int32, (per_req, 1), 0), STEPS)
        drafted = draft_ref[a].astype(jnp.float32)
        drafted = jnp.concatenate(
            [drafted, jnp.zeros((16 - STEPS, drafted.shape[1]), jnp.float32)], axis=0
        ).astype(jnp.bfloat16)
        for h in range(heads):
            q = q_here[h, a * per_req : (a + 1) * per_req, :]
            base = 2 * h * HD
            keys = cache_buf[a, :, base : base + HD]
            values = cache_buf[a, :, base + HD : base + 2 * HD]
            over = (((1,), (1,)), ((), ()))
            sc = lax.dot_general(q, keys, over, preferred_element_type=jnp.float32) * scale
            ok = lax.broadcasted_iota(jnp.int32, sc.shape, 1) < len_ref[a]
            sc = jnp.where(ok, sc, -1e30)
            dk = drafted[:, base : base + HD]
            dv = drafted[:, base + HD : base + 2 * HD]
            sd = lax.dot_general(q, dk, over, preferred_element_type=jnp.float32) * scale
            seen = lax.broadcasted_iota(jnp.int32, sd.shape, 1) <= step_row
            sd = jnp.where(seen, sd, -1e30)
            top = jnp.maximum(
                jnp.max(sc, axis=1, keepdims=True), jnp.max(sd, axis=1, keepdims=True)
            )
            wc = jnp.where(ok, jnp.exp(sc - top), 0.0)
            wd = jnp.where(seen, jnp.exp(sd - top), 0.0)
            total = jnp.sum(wc, axis=1, keepdims=True) + jnp.sum(wd, axis=1, keepdims=True)
            out = jnp.dot(wc.astype(jnp.bfloat16), values, preferred_element_type=jnp.float32)
            out = out + jnp.dot(wd.astype(jnp.bfloat16), dv, preferred_element_type=jnp.float32)
            at = pl.ds(a * per_req, per_req)
            cache_out[h, at, :] = out
            cache_ml[h, at, :] = pack(top, total)

    def unpack(packed):
        wide_row = jnp.broadcast_to(packed[0:1, :], (rows, LANES))
        at = lax.broadcasted_iota(jnp.int32, wide_row.shape, 1)
        mine = lax.broadcasted_iota(jnp.int32, wide_row.shape, 0)
        return [
            jnp.sum(jnp.where(at == mine + off, wide_row, 0.0), axis=1, keepdims=True)
            for off in (0, LANES // 2)
        ]

    def factors(h):
        stats = [(cache_ml[h, :, 0:1], cache_ml[h, :, LANES - 1 : LANES]), unpack(ml_send[h, w])]
        for d in range(1, n):
            s = lax.rem(w + d, n)
            state_copy(h, d, s, False).wait_recv()
            stats.append(unpack(ml_recv[h, s]))
        top = functools.reduce(jnp.maximum, [each[0] for each in stats])
        scaled = [jnp.exp(each[0] - top) for each in stats]
        total = sum(f * each[1] for f, each in zip(scaled, stats))
        return [f / total for f in scaled]

    def merge(h, share):
        out = share[0] * cache_out[h] + share[1] * out_send[h, w].astype(jnp.float32)
        for d in range(1, n):
            s = lax.rem(w + d, n)
            state_copy(h, d, s, True).wait_recv()
            out = out + share[d + 1] * out_recv[h, s].astype(jnp.float32)
        for a in range(req_dev):
            for g in range(groups):
                at = (a * groups + g) * STEPS
                cut = slice((h * groups + g) * HD, (h * groups + g + 1) * HD)
                out_ref[a, :, cut] = out[at : at + STEPS, :].astype(out_ref.dtype)

    send_own(0, 0)
    for h in range(heads):
        q_here[h] = jnp.concatenate(
            [
                query_ref[a, :, (h * groups + g) * HD : (h * groups + g + 1) * HD].astype(
                    jnp.float32
                )
                for a in range(req_dev)
                for g in range(groups)
            ],
            axis=0,
        ).astype(jnp.bfloat16)
    for d in range(1, n):
        q_copy(d).start()
    q_all[w] = q_here[...]
    blocks = owner_ref.shape[0]
    shape = (blocks, blocks)
    same = lax.broadcasted_iota(jnp.int32, shape, 0) == lax.broadcasted_iota(jnp.int32, shape, 1)
    request = jnp.sum(jnp.where(same, request_ref[...], 0), axis=1, keepdims=True)
    admit = jnp.sum(jnp.where(same, admit_ref[...], 0), axis=1, keepdims=True)
    label = jnp.where(admit == 1, owner_ref[...] * req_dev + request, -1)
    shape = (blocks, tokens)
    block_of = lax.broadcasted_iota(jnp.int32, shape, 1) // (tokens // blocks)
    inside = block_of == lax.broadcasted_iota(jnp.int32, shape, 0)
    row = jnp.sum(jnp.where(inside, label, 0), axis=0, keepdims=True)
    labels[...] = jnp.broadcast_to(row, labels.shape)
    x_copy.wait()
    strip = min(64, tokens)

    @pl.loop(0, tokens // strip)
    def _(i):
        at = pl.ds(pl.multiple_of(i * strip, strip), strip)
        sums = jnp.zeros((strip, LANES), jnp.float32)
        for c in range(depth // LANES):
            cut = slice(c * LANES, (c + 1) * LANES)
            piece = xbuf[at, cut].astype(jnp.float32)
            sums = sums + piece * piece
            xbuf[at, cut] = (piece * gain_ref[:, cut]).astype(jnp.bfloat16)
        squares_here[at, :] = sums

    for d in range(1, m_count):
        sq_copy(d, me).start()

    order = [(r, k) for r in range(rounds) for k in range(pieces)]

    def stats():
        total = squares_here[...]
        for d in range(1, m_count):
            s = lax.rem(me + d, m_count)
            sq_copy(d, s).wait_recv()
            total = total + squares[s]
        mean = jnp.sum(total, axis=1, keepdims=True) / D
        inverse[...] = jnp.broadcast_to(lax.rsqrt(mean + 1e-05), inverse.shape)
        for d in range(1, n):
            q_arrival(d).wait_recv()

    def collect(r):
        reduce(r)
        if r % 2 == 0:
            attend_scores(r // 2)
        else:
            attend_values(r // 2)

    work = {}

    def plan(r, k, job):
        work.setdefault((r, min(k, pieces - 1)), []).append(job)

    for a in range(req_dev):
        plan(0, a, functools.partial(attend_cache, a))
    for r in range(1, rounds):
        plan(r, 0, functools.partial(multiply, r - 1))
        if r == 1:
            plan(r, 0, stats)
        else:
            plan(r, 1, functools.partial(collect, r - 2))
    cache_copy.wait()
    for i, (r, k) in enumerate(order):
        if i + 1 < len(order):
            send_own(*order[i + 1])
        relay(r, k)
        for job in work.get((r, k), []):
            job()
    multiply(rounds - 1)
    for r in range(max(rounds - 2, 0), rounds):
        collect(r)
    shares = [factors(h) for h in range(heads)]
    for h in range(heads):
        merge(h, shares[h])

    for r, k in order:
        for step in (1, -1):

            @pl.when(has_next(step))
            def _():
                own_send(r, k, step).wait_send()

        for d in range(1, n):
            for step in (1, -1):

                @pl.when(has_source(d, step))
                def _():
                    s = w - d * step

                    @pl.when(has_next(step))
                    def _():
                        forward(r, k, s, step).wait_send()

                    across(r, k, s, side).wait_send()

    for r in range(rounds):
        for d in range(1, m_count):
            rs_copy(r, d, me).wait_send()
    for d in range(1, n):
        q_copy(d).wait_send()
        for h in range(heads):
            state_copy(h, d, w, False).wait_send()
            state_copy(h, d, w, True).wait_send()
    for d in range(1, m_count):
        sq_copy(d, me).wait_send()


def on_device_fused(
    mesh,
    prompt_states,
    norm_gain,
    kv_weight,
    block_owner,
    block_request,
    block_admit,
    cache_kv,
    cache_len,
    queries,
    draft_kv,
):
    n, m_count = mesh.shape["wide"], mesh.shape["mp"]
    tokens, depth = prompt_states.shape
    columns = kv_weight.shape[1]
    req_dev, cached, width = cache_kv.shape
    groups = QH // KVH
    rows = req_dev * STEPS * groups
    plain = mesh.shape["parts"] != 2 or n != m_count or columns % (2 * HD) or HD != LANES
    if plain or 2 * rows > LANES:
        return on_device(
            prompt_states,
            norm_gain,
            kv_weight,
            block_owner,
            block_request,
            block_admit,
            cache_kv,
            cache_len,
            queries,
            draft_kv,
        )
    rounds = columns // LANES
    heads = width // (2 * HD)
    pieces = 2
    f32, bf16 = jnp.float32, jnp.bfloat16
    vmem = pl.BlockSpec(memory_space=pltpu.VMEM)
    anywhere = pl.BlockSpec(memory_space=pl.ANY)
    dma = pltpu.SemaphoreType.DMA
    return pl.pallas_call(
        functools.partial(fused_kernel, (n, m_count, rounds, heads, req_dev, pieces)),
        out_shape=jax.ShapeDtypeStruct(queries.shape, bf16),
        in_specs=[
            anywhere,
            vmem,
            anywhere,
            vmem,
            vmem,
            vmem,
            anywhere,
            pl.BlockSpec(memory_space=pltpu.SMEM),
            vmem,
            vmem,
        ],
        out_specs=vmem,
        scratch_shapes=[
            pltpu.VMEM((tokens, depth), bf16),
            pltpu.VMEM((rounds, depth, n * LANES), bf16),
            pltpu.VMEM((rounds, m_count, tokens, LANES), bf16),
            pltpu.VMEM((rounds, m_count, tokens, LANES), bf16),
            pltpu.VMEM((tokens, LANES), f32),
            pltpu.VMEM((m_count, tokens, LANES), f32),
            pltpu.VMEM((tokens, LANES), f32),
            pltpu.VMEM((rounds, tokens, LANES), bf16),
            pltpu.VMEM((req_dev, cached, width), bf16),
            pltpu.VMEM((heads, rows, HD), bf16),
            pltpu.VMEM((n, heads, rows, HD), bf16),
            pltpu.VMEM((8, tokens), jnp.int32),
            pltpu.VMEM((heads, n * rows, tokens), bf16),
            pltpu.VMEM((heads, rows, HD), f32),
            pltpu.VMEM((heads, rows, LANES), f32),
            pltpu.VMEM((heads, n, rows, HD), bf16),
            pltpu.VMEM((heads, n, rows, HD), bf16),
            pltpu.VMEM((heads, n, 8, LANES), f32),
            pltpu.VMEM((heads, n, 8, LANES), f32),
            dma((2,)),
            dma((rounds,)),
            dma((rounds * pieces, n)),
            dma((rounds * pieces, n)),
            dma((rounds * pieces, n)),
            dma((rounds * pieces, n)),
            dma((rounds * pieces, n)),
            dma((n,)),
            dma((n,)),
            dma((m_count,)),
            dma((m_count,)),
            dma((rounds, m_count)),
            dma((rounds, m_count)),
            dma((heads, n)),
            dma((heads, n)),
            dma((heads, n)),
            dma((heads, n)),
        ],
        compiler_params=pltpu.CompilerParams(
            collective_id=0, has_side_effects=True, vmem_limit_bytes=60 << 20
        ),
    )(
        prompt_states,
        norm_gain[None, :],
        kv_weight,
        block_owner,
        block_request[None, :],
        block_admit[None, :],
        cache_kv,
        cache_len,
        queries,
        draft_kv,
    )


def solution(mesh):
    placed = (
        P(("parts", "wide"), "mp"),
        P("mp"),
        P("mp", "wide"),
        P(("parts", "wide"), None),
        P(("parts", "wide")),
        P(("parts", "wide")),
        P(("parts", "wide"), None, "mp"),
        P(("parts", "wide")),
        P(("parts", "wide"), None, "mp"),
        P(("parts", "wide"), None, "mp"),
    )
    return jax.shard_map(
        functools.partial(on_device_fused, mesh),
        mesh=mesh,
        in_specs=placed,
        out_specs=P(("parts", "wide"), None, "mp"),
        check_vma=False,
    )
```
